32 devices in a mesh: lat: 4 (over y, core), lon: 8 (over z, x).
Axes of the slice: x: 2, y: 2, z: 4, core: 2. Of those that a mesh axis runs over, the one named last changes fastest.
Arguments:
- tracers: bfloat16 [10, 4, 64, 1024], P(None, None, 'lat', 'lon'), may hold values from -6 to 6
- winds: float32 [3, 4, 64, 1024], P(None, None, 'lat', 'lon'), may hold values from -2.5 to 2.5
- zonal_shift: int32 [64], P('lat'), may hold values from 0 to 1023
Outputs:
- new_tracers: bfloat16 [10, 4, 64, 1024], P(None, None, 'lat', 'lon')
- displacement: float32 [3, 4, 64, 1024], P(None, None, 'lat', 'lon')
The draws below stay inside these ranges and needn't reach their ends.
All inputs are finite; a program needn't handle non-finite values.
Results may differ from the reference program's by a relative error of at most 0.001.
Values may be sent and summed in bfloat16 or wider, within the bound.
A program may use at most 64 MiB of HBM per device.

```python
import jax
import jax.numpy as jnp
from jax import lax

NTR = 10
LEV = 4
ITERS = 3
NLAT = 64
NLON = 1024


def plant(drawn, own_key, least, largest):
    index_at = [jax.random.randint(jax.random.fold_in(own_key, axis), (), 0, length) for axis, length in enumerate(drawn.shape)]
    longest = drawn.shape.index(max(drawn.shape))
    beside = index_at[:longest] + [(index_at[longest] + 1) % drawn.shape[longest]] + index_at[longest + 1:]
    return drawn.at[tuple(index_at)].set(least).at[tuple(beside)].set(largest)


def steps_of(own_key, extent, pieces, least, high):
    def one(position, shards_of):
        heights = jax.random.uniform(jax.random.fold_in(jax.random.fold_in(own_key, 6), position), (shards_of,), jnp.float32, least / len(pieces), high / len(pieces))
        return jnp.repeat(jnp.exp(heights), extent[position] // shards_of).reshape((-1,) + (1,) * (len(extent) - position - 1))

    factor_of = one(*pieces[0])
    for cut in pieces[1:]:
        factor_of = factor_of * one(*cut)
    return factor_of


def gaussian(rng, extent, spread, limit, split=(), held_as=jnp.bfloat16):
    drawn = jax.random.normal(rng, extent, jnp.float32) * spread
    if len(split) > 0:
        drawn = steps_of(rng, extent, split, -0.22, 0.18) * drawn
    return jnp.clip(drawn, min=-limit, max=limit).astype(held_as)


def setup_inputs(seed: int = 0) -> dict:
    key_of = jax.random.split(jax.random.key(seed), 4)
    tracers = gaussian(key_of[0], (NTR, LEV, NLAT, NLON), 1.0, 6.0, ((2, 4), (3, 8)))
    winds = jnp.clip(jax.random.uniform(key_of[1], (3, LEV, NLAT, NLON), jnp.float32, -2.5, 2.5) * steps_of(key_of[1], (3, LEV, NLAT, NLON), ((2, 4), (3, 8)), -0.4, 0.0), -2.5, 2.5)
    zonal_shift = plant(jax.random.randint(key_of[2], (NLAT,), 0, NLON), jax.random.fold_in(key_of[2], 1), 0, NLON - 1).astype(jnp.int32)
    return dict(tracers=tracers, winds=winds, zonal_shift=zonal_shift)


def cubic_weights(frac):
    return (-frac * (frac - 1.0) * (frac - 2.0) / 6.0,
            (frac + 1.0) * (frac - 1.0) * (frac - 2.0) / 2.0,
            -(frac + 1.0) * frac * (frac - 2.0) / 2.0,
            (frac + 1.0) * frac * (frac - 1.0) / 6.0)


def reference(tracers, winds, zonal_shift):
    shape = (LEV, NLAT, NLON)
    kpos = lax.broadcasted_iota(jnp.float32, shape, 0)
    gpos = lax.broadcasted_iota(jnp.float32, shape, 1)
    jcol = lax.broadcasted_iota(jnp.int32, shape, 2)
    wide = jnp.pad(winds, ((0, 0), (1, 1), (2, 2), (0, 0))).reshape(3, -1)

    def wind_at(disp):
        zlev = jnp.clip(kpos - 0.5 * disp[0], 0.0, LEV - 1.0)
        ylat = jnp.clip(gpos - 0.5 * disp[1], 0.0, NLAT - 1.0)
        xrel = -0.5 * disp[2]
        zb = jnp.floor(zlev)
        yb = jnp.floor(ylat)
        xb = jnp.floor(xrel)
        tz = zlev - zb
        ty = ylat - yb
        tx = xrel - xb
        zi = zb.astype(jnp.int32) + 1
        yi = yb.astype(jnp.int32) + 2
        xi = jcol + xb.astype(jnp.int32)
        wz = (1.0 - tz, tz)
        wy = (1.0 - ty, ty)
        wx = (1.0 - tx, tx)
        total = jnp.zeros((3,) + shape, jnp.float32)
        for a in range(2):
            for b in range(2):
                for c in range(2):
                    index = ((zi + a) * (NLAT + 4) + (yi + b)) * NLON + jnp.mod(xi + c, NLON)
                    picked = jnp.take(wide, index.reshape(-1), axis=1).reshape((3,) + shape)
                    total = total + (wz[a] * wy[b] * wx[c]) * picked
        return total

    disp = winds
    for step in range(ITERS):
        disp = wind_at(disp)

    colrow = lax.broadcasted_iota(jnp.int32, (NLAT, NLON), 1)
    source_col = jnp.mod(colrow - zonal_shift[:, None], NLON).astype(jnp.int32)
    source_col = jnp.broadcast_to(source_col[None, None], tracers.shape)
    moved = jnp.take_along_axis(tracers, source_col, axis=3)

    zdep = jnp.clip(kpos - disp[0], 0.0, LEV - 1.0)
    ydep = jnp.clip(gpos - disp[1], 0.0, NLAT - 1.0)
    xrel = -disp[2]
    zb = jnp.floor(zdep)
    yb = jnp.floor(ydep)
    xb = jnp.floor(xrel)
    wz = cubic_weights(zdep - zb)
    wy = cubic_weights(ydep - yb)
    wx = cubic_weights(xrel - xb)
    zi = zb.astype(jnp.int32) + 1
    yi = yb.astype(jnp.int32) + 1
    base_col = jcol + xb.astype(jnp.int32) - 1
    padded = jnp.pad(moved, ((0, 0), (2, 2), (2, 2), (0, 0))).reshape(NTR, -1)
    result = jnp.zeros((NTR,) + shape, jnp.float32)
    for a in range(4):
        for b in range(4):
            partial_value = jnp.zeros((NTR,) + shape, jnp.float32)
            for c in range(4):
                index = ((zi + a) * (NLAT + 4) + (yi + b)) * NLON + jnp.mod(base_col + c, NLON)
                picked = jnp.take(padded, index.reshape(-1), axis=1).reshape((NTR,) + shape)
                partial_value = partial_value + wx[c] * picked
            result = result + (wz[a] * wy[b]) * partial_value
    return result.astype(jnp.bfloat16), disp
```

```python
import functools

import jax
import jax.numpy as jnp
from jax import lax
from jax.experimental import pallas as pl
from jax.experimental.pallas import tpu as pltpu
from jax.sharding import PartitionSpec as P

ITERS = 3
RIM = 4
SUB = 8
MESH = pl.DeviceIdType.MESH


def cubic_weights(frac):
    return (
        -frac * (frac - 1.0) * (frac - 2.0) / 6.0,
        (frac + 1.0) * (frac - 1.0) * (frac - 2.0) / 2.0,
        -(frac + 1.0) * frac * (frac - 2.0) / 2.0,
        (frac + 1.0) * frac * (frac - 1.0) / 6.0,
    )


def spread(base, weights, lowest, highest):
    listed = []
    for target in range(lowest, highest + 1):
        summed = jnp.zeros(base.shape, jnp.float32)
        for a in range(len(weights)):
            summed = summed + jnp.where(base == float(target - a), weights[a], 0.0)
        listed.append(summed)
    return listed


def exchange_kernel(
    nlat, nlon, levels, t_ref, w_ref, s_ref, g_ref, s_out, d_ref,
    edge, edges, wind_n, wind_s, wide,
    sem_z, sem_x, sem_n, sem_s, got, got_n, got_s, own_sem,
    sem_w, got_w, sem_i, got_i,
):
    rows, _, cols = t_ref.shape
    planes = w_ref.shape[0]
    lat = lax.axis_index("lat")
    lon = lax.axis_index("lon")
    zc = nlon // 2
    zi = lon // 2
    xi = lon % 2
    north = (lat + nlat - 1) % nlat
    south = (lat + 1) % nlat
    east = (lon + 1) % nlon
    west = (lon + nlon - 1) % nlon
    partner = zi * 2 + (1 - xi)

    def peer(j):
        return ((zi + j) % zc) * 2 + xi

    around = [(lat, east), (lat, west), (north, east), (north, west), (south, east), (south, west)]
    targets = [(north, lon), (south, lon), (lat, partner)] + around
    targets += [(lat, peer(j)) for j in range(1, zc)]
    barrier = pltpu.get_barrier_semaphore()
    for target in targets:
        pl.semaphore_signal(barrier, inc=1, device_id=target, device_id_type=MESH)

    lane = lax.broadcasted_iota(jnp.int32, (rows, cols), 1)
    packed = jnp.zeros((rows, cols), jnp.float32)
    for c in range(planes):
        turned = pltpu.roll(w_ref[c], (2 + 4 * c) % cols, 1)
        packed = jnp.where((lane >= 4 * c) & (lane < 4 * c + 4), turned, packed)
    edge[...] = packed
    s_out[RIM : RIM + rows] = s_ref[...]
    pl.semaphore_wait(barrier, len(targets))

    def remote(src, dst, send, recv, target):
        copy = pltpu.make_async_remote_copy(
            src_ref=src, dst_ref=dst, send_sem=send, recv_sem=recv,
            device_id=target, device_id_type=MESH,
        )
        copy.start()
        return copy

    sends = []
    winds = []
    for n, target in enumerate(around):
        slot = (1, 0, 5, 4, 3, 2)[n]
        winds.append(remote(edge, edges.at[slot], sem_w.at[n], got_w.at[slot], target))
    winds.append(remote(w_ref.at[:, 0:SUB], wind_s, sem_w.at[6], got_w.at[6], (north, lon)))
    winds.append(remote(w_ref.at[:, rows - SUB : rows], wind_n, sem_w.at[7], got_w.at[7], (south, lon)))
    winds.append(remote(s_ref.at[0:RIM], s_out.at[RIM + rows : RIM + rows + RIM], sem_i.at[0], got_i.at[0], (north, lon)))
    winds.append(remote(s_ref.at[rows - RIM : rows], s_out.at[0:RIM], sem_i.at[1], got_i.at[1], (south, lon)))

    body = pl.ds(RIM, rows)
    sends.append(remote(t_ref, g_ref.at[lon, body], sem_x.at[lon], got.at[lon], (lat, partner)))
    for j in [j for pair in zip(range(1, zc), range(zc - 1, 0, -1)) for j in pair][: zc - 1]:
        sends.append(remote(t_ref, g_ref.at[lon, body], sem_z.at[j], got.at[lon], (lat, peer(j))))

    def rims(p, src, first):
        sends.append(remote(src.at[first : first + RIM], g_ref.at[p, RIM + rows : RIM + rows + RIM], sem_n.at[p], got_n.at[p], (north, lon)))
        sends.append(remote(src.at[first + rows - RIM : first + rows], g_ref.at[p, 0:RIM], sem_s.at[p], got_s.at[p], (south, lon)))

    rims(lon, t_ref, 0)
    own = pltpu.make_async_copy(t_ref, g_ref.at[lon, body], own_sem)
    own.start()

    def arrived(p):
        pltpu.make_async_remote_copy(
            src_ref=g_ref.at[p, body], dst_ref=g_ref.at[p, body], send_sem=own_sem, recv_sem=got.at[p],
            device_id=(lat, partner), device_id_type=MESH,
        ).wait_recv()

    def relay(j):
        p = ((zi + zc - j) % zc) * 2 + xi
        arrived(p)
        sends.append(remote(g_ref.at[p, body], g_ref.at[p, body], sem_x.at[p], got.at[p], (lat, partner)))
        rims(p, g_ref.at[p], RIM)

    def pass_rims(j):
        p = ((zi + zc - j) % zc) * 2 + (1 - xi)
        arrived(p)
        rims(p, g_ref.at[p], RIM)

    for copy in winds:
        copy.wait()

    tall = rows + 2 * SUB
    total_rows = rows * nlat
    tall_lane = lax.broadcasted_iota(jnp.int32, (tall, cols), 1)
    rowpos = lax.broadcasted_iota(jnp.int32, (tall, cols), 0) + (lat * rows - SUB)
    inside = (rowpos >= 0) & (rowpos < total_rows)
    from_east = jnp.concatenate([edges[2][rows - SUB :], edges[0], edges[4][:SUB]], axis=0)
    from_west = jnp.concatenate([edges[3][rows - SUB :], edges[1], edges[5][:SUB]], axis=0)
    for c in range(planes):
        block = jnp.concatenate([wind_n[c], w_ref[c], wind_s[c]], axis=0)
        for d in range(-2, 3):
            if d > 0:
                value = jnp.where(
                    tall_lane >= cols - d,
                    pltpu.roll(from_east, (cols - 2 - d - 4 * c) % cols, 1),
                    pltpu.roll(block, cols - d, 1),
                )
            elif d < 0:
                value = jnp.where(
                    tall_lane < -d,
                    pltpu.roll(from_west, (-d - 2 - 4 * c) % cols, 1),
                    pltpu.roll(block, -d, 1),
                )
            else:
                value = block
            wide[d + 2, c] = jnp.where(inside, value, 0.0)

    def trajectory(k):
        for b in range(rows // SUB):
            near = slice(b * SUB, (b + 1) * SUB)
            growi = lax.broadcasted_iota(jnp.int32, (SUB, cols), 0) + (lat * rows + b * SUB)
            gpos = growi.astype(jnp.float32)

            def step(_, disp):
                zlev = jnp.clip(float(k) - 0.5 * disp[0], 0.0, levels - 1.0)
                ylat = jnp.clip(gpos - 0.5 * disp[1], 0.0, total_rows - 1.0)
                xrel = -0.5 * disp[2]
                zb = jnp.floor(zlev)
                yb = jnp.floor(ylat)
                xb = jnp.floor(xrel)
                tz = zlev - zb
                ty = ylat - yb
                tx = xrel - xb
                wz = spread(zb, (1.0 - tz, tz), 0, levels - 1)
                wy = spread(yb - gpos, (1.0 - ty, ty), -2, 2)
                wx = spread(xb, (1.0 - tx, tx), -2, 2)
                result = []
                for comp in range(3):
                    total = None
                    for z in range(levels):
                        plane = None
                        for y in range(5):
                            start = SUB + b * SUB + y - 2
                            line = None
                            for x in range(5):
                                term = wx[x] * wide[x, comp * levels + z, start : start + SUB]
                                line = term if line is None else line + term
                            term = wy[y] * line
                            plane = term if plane is None else plane + term
                        term = wz[z] * plane
                        total = term if total is None else total + term
                    result.append(total)
                return tuple(result)

            disp = tuple(w_ref[comp * levels + k, near] for comp in range(3))
            disp = lax.fori_loop(0, ITERS, step, disp)
            for comp in range(3):
                d_ref[comp * levels + k, near] = disp[comp]

    order = [j for pair in zip(range(1, zc), range(zc - 1, 0, -1)) for j in pair][: zc - 1]
    for n in range(max(levels, len(order))):
        if n < len(order):
            relay(order[n])
        if n < levels:
            trajectory(n)
    pass_rims(0)
    for j in order:
        pass_rims(j)
    own.wait()
    for copy in sends:
        copy.wait_send()
    for p in range(nlon):
        for dst, sem in ((g_ref.at[p, RIM + rows : RIM + rows + RIM], got_n), (g_ref.at[p, 0:RIM], got_s)):
            pltpu.make_async_remote_copy(
                src_ref=dst, dst_ref=dst, send_sem=own_sem, recv_sem=sem.at[p],
                device_id=(north, lon), device_id_type=MESH,
            ).wait_recv()


def stencil_kernel(nlat, nlon, levels, rows, s_ref, d_ref, g_ref, o_ref, window, shifted, result, sems):
    high, fields, cols = g_ref.shape[1:]
    ntrac = fields // levels
    lat = lax.axis_index("lat")
    lon = lax.axis_index("lon")
    total_rows = rows * nlat

    def place(r):
        first = lon * cols - RIM - s_ref[r, 0, 0] + 2 * nlon * cols
        return first // cols, first % cols

    def fetch(r, n):
        sector = (place(r)[0] + n) % nlon
        return pltpu.make_async_copy(g_ref.at[sector, r], window.at[r, n], sems.at[r])

    def start(r, _):
        for n in range(3):
            fetch(r, n).start()
        return 0

    lax.fori_loop(0, high, start, 0)
    lane = lax.broadcasted_iota(jnp.int32, (fields, cols), 1)

    def turn(r, _):
        pltpu.make_async_copy(g_ref.at[0:3, r], window.at[r], sems.at[r]).wait()
        offset = place(r)[1]
        rowpos = lat * rows - RIM + r
        inside = (rowpos >= 0) & (rowpos < total_rows)
        amount = (cols - offset) % cols
        turned = [pltpu.roll(window[r, n].astype(jnp.float32), amount, 1) for n in range(3)]
        early = lane < cols - offset
        keep = jnp.full((fields, cols), inside)
        low = jnp.where(keep, jnp.where(early, turned[0], turned[1]), 0.0)
        high_part = jnp.where(keep, jnp.where(early, turned[1], turned[2]), 0.0)
        for d in range(2 * RIM + 1):
            value = low
            if d > 0:
                value = jnp.where(
                    lane < cols - d, pltpu.roll(low, cols - d, 1), pltpu.roll(high_part, cols - d, 1)
                )
            shifted[d, pl.ds(r, fields, stride=high), :] = value
        return 0

    lax.fori_loop(0, high, turn, 0)
    wide = 2 * RIM + 1
    for k in range(levels):
        for b in range(rows // SUB):
            near = slice(b * SUB, (b + 1) * SUB)
            growi = lax.broadcasted_iota(jnp.int32, (SUB, cols), 0) + (lat * rows + b * SUB)
            gpos = growi.astype(jnp.float32)
            zdep = jnp.clip(float(k) - d_ref[k, near], 0.0, levels - 1.0)
            ydep = jnp.clip(gpos - d_ref[levels + k, near], 0.0, total_rows - 1.0)
            xrel = -d_ref[2 * levels + k, near]
            zb = jnp.floor(zdep)
            yb = jnp.floor(ydep)
            xb = jnp.floor(xrel)
            wz = spread(zb - 1.0, cubic_weights(zdep - zb), 0, levels - 1)
            wy = spread(yb - gpos - 1.0, cubic_weights(ydep - yb), -RIM, RIM)
            wx = spread(xb - 1.0, cubic_weights(xrel - xb), -RIM, RIM)

            def tracer(t, _):
                total = None
                for z in range(levels):
                    base = pl.multiple_of((t * levels + z) * high + b * SUB, SUB)
                    plane = None
                    for y in range(wide):
                        line = None
                        for x in range(wide):
                            term = wx[x] * shifted[x, pl.ds(base + y, SUB), :]
                            line = term if line is None else line + term
                        term = wy[y] * line
                        plane = term if plane is None else plane + term
                    term = wz[z] * plane
                    total = term if total is None else total + term
                result[t * levels + k, near] = total
                return 0

            lax.fori_loop(0, ntrac, tracer, 0)
    o_ref[...] = result[...].astype(o_ref.dtype)


def local(tracers, winds, zonal_shift):
    ntrac, levels, rows, cols = tracers.shape
    nlat = lax.axis_size("lat")
    nlon = lax.axis_size("lon")
    fields = ntrac * levels
    planes = 3 * levels
    high = rows + 2 * RIM
    dma = pltpu.SemaphoreType.DMA
    vmem = pl.BlockSpec(memory_space=pltpu.VMEM)
    any_space = pl.BlockSpec(memory_space=pl.ANY)
    by_row = jnp.transpose(tracers.reshape(fields, rows, cols), (1, 0, 2))
    shift_rows = jnp.broadcast_to(zonal_shift[:, None, None], (rows, 1, 128))
    gathered, shifts, disp = pl.pallas_call(
        functools.partial(exchange_kernel, nlat, nlon, levels),
        out_shape=(
            jax.ShapeDtypeStruct((nlon, high, fields, cols), tracers.dtype),
            jax.ShapeDtypeStruct((high, 1, 128), jnp.int32),
            jax.ShapeDtypeStruct((planes, rows, cols), jnp.float32),
        ),
        in_specs=[vmem, vmem, vmem],
        out_specs=(any_space, vmem, vmem),
        scratch_shapes=[
            pltpu.VMEM((rows, cols), jnp.float32),
            pltpu.VMEM((6, rows, cols), jnp.float32),
            pltpu.VMEM((planes, SUB, cols), jnp.float32),
            pltpu.VMEM((planes, SUB, cols), jnp.float32),
            pltpu.VMEM((5, planes, rows + 2 * SUB, cols), jnp.float32),
            dma((nlon,)), dma((nlon,)), dma((nlon,)), dma((nlon,)),
            dma((nlon,)), dma((nlon,)), dma((nlon,)), dma,
            dma((8,)), dma((8,)), dma((2,)), dma((2,)),
        ],
        compiler_params=pltpu.CompilerParams(collective_id=0, has_side_effects=True),
        name="exchange",
    )(by_row, winds.reshape(planes, rows, cols), shift_rows)
    out = pl.pallas_call(
        functools.partial(stencil_kernel, nlat, nlon, levels, rows),
        out_shape=jax.ShapeDtypeStruct((fields, rows, cols), tracers.dtype),
        in_specs=[pl.BlockSpec(memory_space=pltpu.SMEM), vmem, any_space],
        out_specs=vmem,
        scratch_shapes=[
            pltpu.VMEM((high, 3, fields, cols), tracers.dtype),
            pltpu.VMEM((2 * RIM + 1, fields * high, cols), jnp.float32),
            pltpu.VMEM((fields, rows, cols), jnp.float32),
            dma((high,)),
        ],
        name="stencil",
    )(shifts, disp, gathered)
    return out.reshape(tracers.shape), disp.reshape(winds.shape)


def solution(mesh):
    return jax.shard_map(
        local,
        mesh=mesh,
        in_specs=(P(None, None, "lat", "lon"), P(None, None, "lat", "lon"), P("lat")),
        out_specs=(P(None, None, "lat", "lon"), P(None, None, "lat", "lon")),
        check_vma=False,
    )
```

```python
import functools

import jax
import jax.numpy as jnp
from jax import lax
from jax.experimental import pallas as pl
from jax.experimental.pallas import tpu as pltpu
from jax.sharding import PartitionSpec as P

ITERS = 3
RIM = 4
SUB = 8
MESH = pl.DeviceIdType.MESH


def cubic_weights(frac):
    return (
        -frac * (frac - 1.0) * (frac - 2.0) / 6.0,
        (frac + 1.0) * (frac - 1.0) * (frac - 2.0) / 2.0,
        -(frac + 1.0) * frac * (frac - 2.0) / 2.0,
        (frac + 1.0) * frac * (frac - 1.0) / 6.0,
    )


def spread(base, weights, lowest, highest):
    listed = []
    for target in range(lowest, highest + 1):
        summed = jnp.zeros(base.shape, jnp.float32)
        for a in range(len(weights)):
            summed = summed + jnp.where(base == float(target - a), weights[a], 0.0)
        listed.append(summed)
    return listed


def exchange_kernel(
    nlat, nlon, levels, t_ref, w_ref, s_ref, g_ref, s_out, d_ref,
    edge, edges, wind_n, wind_s, wide,
    sem_z, sem_x, sem_n, sem_s, got, got_n, got_s, own_sem,
    sem_w, got_w, sem_i, got_i,
):
    rows, _, cols = t_ref.shape
    planes = w_ref.shape[0]
    lat = lax.axis_index("lat")
    lon = lax.axis_index("lon")
    zc = nlon // 2
    zi = lon // 2
    xi = lon % 2
    north = (lat + nlat - 1) % nlat
    south = (lat + 1) % nlat
    east = (lon + 1) % nlon
    west = (lon + nlon - 1) % nlon
    partner = zi * 2 + (1 - xi)

    def peer(j):
        return ((zi + j) % zc) * 2 + xi

    around = [(lat, east), (lat, west), (north, east), (north, west), (south, east), (south, west)]
    targets = [(north, lon), (south, lon), (lat, partner)] + around
    targets += [(lat, peer(j)) for j in range(1, zc)]
    barrier = pltpu.get_barrier_semaphore()
    for target in targets:
        pl.semaphore_signal(barrier, inc=1, device_id=target, device_id_type=MESH)

    lane = lax.broadcasted_iota(jnp.int32, (rows, cols), 1)
    packed = jnp.zeros((rows, cols), jnp.float32)
    for c in range(planes):
        turned = pltpu.roll(w_ref[c], (2 + 4 * c) % cols, 1)
        packed = jnp.where((lane >= 4 * c) & (lane < 4 * c + 4), turned, packed)
    edge[...] = packed
    for r in range(rows):
        s_out[RIM + r] = jnp.full(s_out.shape[1:], s_ref[r])
    pl.semaphore_wait(barrier, len(targets))

    def remote(src, dst, send, recv, target):
        copy = pltpu.make_async_remote_copy(
            src_ref=src, dst_ref=dst, send_sem=send, recv_sem=recv,
            device_id=target, device_id_type=MESH,
        )
        copy.start()
        return copy

    sends = []
    winds = []
    for n, target in enumerate(around):
        slot = (1, 0, 5, 4, 3, 2)[n]
        winds.append(remote(edge, edges.at[slot], sem_w.at[n], got_w.at[slot], target))
    winds.append(remote(w_ref.at[:, 0:SUB], wind_s, sem_w.at[6], got_w.at[6], (north, lon)))
    winds.append(remote(w_ref.at[:, rows - SUB : rows], wind_n, sem_w.at[7], got_w.at[7], (south, lon)))
    own_rows = s_out.at[RIM : RIM + rows]
    winds.append(remote(own_rows.at[0:RIM], s_out.at[RIM + rows : RIM + rows + RIM], sem_i.at[0], got_i.at[0], (north, lon)))
    winds.append(remote(own_rows.at[rows - RIM : rows], s_out.at[0:RIM], sem_i.at[1], got_i.at[1], (south, lon)))

    pieces = rows // RIM
    piece_order = [0, pieces - 1] + list(range(1, pieces - 1))
    order = [j for pair in zip(range(1, zc), range(zc - 1, 0, -1)) for j in pair][: zc - 1]

    def part(c):
        return pl.ds(RIM + c * RIM, RIM)

    def rims(p, c, src):
        if c == 0:
            sends.append(remote(src, g_ref.at[p, RIM + rows : RIM + rows + RIM], sem_n.at[p], got_n.at[p], (north, lon)))
        if c == pieces - 1:
            sends.append(remote(src, g_ref.at[p, 0:RIM], sem_s.at[p], got_s.at[p], (south, lon)))

    for c in piece_order:
        mine = t_ref.at[c * RIM : (c + 1) * RIM]
        sends.append(remote(mine, g_ref.at[lon, part(c)], sem_x.at[lon, c], got.at[lon, c], (lat, partner)))
        for j in order:
            sends.append(remote(mine, g_ref.at[lon, part(c)], sem_z.at[j, c], got.at[lon, c], (lat, peer(j))))
        rims(lon, c, mine)
    own = pltpu.make_async_copy(t_ref, g_ref.at[lon, RIM : RIM + rows], own_sem)
    own.start()

    def arrived(p, c):
        pltpu.make_async_remote_copy(
            src_ref=g_ref.at[p, part(c)], dst_ref=g_ref.at[p, part(c)], send_sem=own_sem, recv_sem=got.at[p, c],
            device_id=(lat, partner), device_id_type=MESH,
        ).wait_recv()

    def relay(c):
        for j in order:
            p = ((zi + zc - j) % zc) * 2 + xi
            arrived(p, c)
            piece = g_ref.at[p, part(c)]
            sends.append(remote(piece, piece, sem_x.at[p, c], got.at[p, c], (lat, partner)))
            rims(p, c, piece)

    def pass_rims(c):
        for j in [0] + order:
            p = ((zi + zc - j) % zc) * 2 + (1 - xi)
            arrived(p, c)
            rims(p, c, g_ref.at[p, part(c)])

    for copy in winds:
        copy.wait()

    tall = rows + 2 * SUB
    total_rows = rows * nlat
    tall_lane = lax.broadcasted_iota(jnp.int32, (tall, cols), 1)
    rowpos = lax.broadcasted_iota(jnp.int32, (tall, cols), 0) + (lat * rows - SUB)
    inside = (rowpos >= 0) & (rowpos < total_rows)
    from_east = jnp.concatenate([edges[2][rows - SUB :], edges[0], edges[4][:SUB]], axis=0)
    from_west = jnp.concatenate([edges[3][rows - SUB :], edges[1], edges[5][:SUB]], axis=0)
    for c in range(planes):
        block = jnp.concatenate([wind_n[c], w_ref[c], wind_s[c]], axis=0)
        for d in range(-2, 3):
            if d > 0:
                value = jnp.where(
                    tall_lane >= cols - d,
                    pltpu.roll(from_east, (cols - 2 - d - 4 * c) % cols, 1),
                    pltpu.roll(block, cols - d, 1),
                )
            elif d < 0:
                value = jnp.where(
                    tall_lane < -d,
                    pltpu.roll(from_west, (-d - 2 - 4 * c) % cols, 1),
                    pltpu.roll(block, -d, 1),
                )
            else:
                value = block
            wide[d + 2, c] = jnp.where(inside, value, 0.0)

    def trajectory(k):
        for b in range(rows // SUB):
            near = slice(b * SUB, (b + 1) * SUB)
            growi = lax.broadcasted_iota(jnp.int32, (SUB, cols), 0) + (lat * rows + b * SUB)
            gpos = growi.astype(jnp.float32)

            def step(_, disp):
                zlev = jnp.clip(float(k) - 0.5 * disp[0], 0.0, levels - 1.0)
                ylat = jnp.clip(gpos - 0.5 * disp[1], 0.0, total_rows - 1.0)
                xrel = -0.5 * disp[2]
                zb = jnp.floor(zlev)
                yb = jnp.floor(ylat)
                xb = jnp.floor(xrel)
                tz = zlev - zb
                ty = ylat - yb
                tx = xrel - xb
                wz = spread(zb, (1.0 - tz, tz), 0, levels - 1)
                wy = spread(yb - gpos, (1.0 - ty, ty), -2, 2)
                wx = spread(xb, (1.0 - tx, tx), -2, 2)
                result = []
                for comp in range(3):
                    total = None
                    for z in range(levels):
                        plane = None
                        for y in range(5):
                            start = SUB + b * SUB + y - 2
                            line = None
                            for x in range(5):
                                term = wx[x] * wide[x, comp * levels + z, start : start + SUB]
                                line = term if line is None else line + term
                            term = wy[y] * line
                            plane = term if plane is None else plane + term
                        term = wz[z] * plane
                        total = term if total is None else total + term
                    result.append(total)
                return tuple(result)

            disp = tuple(w_ref[comp * levels + k, near] for comp in range(3))
            disp = lax.fori_loop(0, ITERS, step, disp)
            for comp in range(3):
                d_ref[comp * levels + k, near] = disp[comp]

    for n in range(max(levels, pieces)):
        if n < levels:
            trajectory(n)
        if n < pieces:
            relay(piece_order[n])
            if n > 0:
                pass_rims(piece_order[n - 1])
    pass_rims(piece_order[-1])
    own.wait()
    for copy in sends:
        copy.wait_send()
    for p in range(nlon):
        for dst, sem in ((g_ref.at[p, RIM + rows : RIM + rows + RIM], got_n), (g_ref.at[p, 0:RIM], got_s)):
            pltpu.make_async_remote_copy(
                src_ref=dst, dst_ref=dst, send_sem=own_sem, recv_sem=sem.at[p],
                device_id=(north, lon), device_id_type=MESH,
            ).wait_recv()


def stencil_kernel(nlat, nlon, levels, rows, s_ref, d_ref, g_ref, o_ref, window, shifted, result, sems):
    high, fields, cols = g_ref.shape[1:]
    ntrac = fields // levels
    lat = lax.axis_index("lat")
    lon = lax.axis_index("lon")
    total_rows = rows * nlat

    def place(r):
        first = lon * cols - RIM - s_ref[r, 0, 0] + 2 * nlon * cols
        return first // cols, first % cols

    def fetch(r, n):
        sector = (place(r)[0] + n) % nlon
        return pltpu.make_async_copy(g_ref.at[sector, r], window.at[r, n], sems.at[r])

    def start(r, _):
        for n in range(3):
            fetch(r, n).start()
        return 0

    lax.fori_loop(0, high, start, 0)
    lane = lax.broadcasted_iota(jnp.int32, (fields, cols), 1)

    def turn(r, _):
        pltpu.make_async_copy(g_ref.at[0:3, r], window.at[r], sems.at[r]).wait()
        offset = place(r)[1]
        rowpos = lat * rows - RIM + r
        inside = (rowpos >= 0) & (rowpos < total_rows)
        amount = (cols - offset) % cols
        turned = [pltpu.roll(window[r, n].astype(jnp.float32), amount, 1) for n in range(3)]
        early = lane < cols - offset
        keep = jnp.full((fields, cols), inside)
        low = jnp.where(keep, jnp.where(early, turned[0], turned[1]), 0.0)
        high_part = jnp.where(keep, jnp.where(early, turned[1], turned[2]), 0.0)
        for d in range(2 * RIM + 1):
            value = low
            if d > 0:
                value = jnp.where(
                    lane < cols - d, pltpu.roll(low, cols - d, 1), pltpu.roll(high_part, cols - d, 1)
                )
            shifted[d, pl.ds(r, fields, stride=high), :] = value
        return 0

    lax.fori_loop(0, high, turn, 0)
    wide = 2 * RIM + 1
    for k in range(levels):
        for b in range(rows // SUB):
            near = slice(b * SUB, (b + 1) * SUB)
            growi = lax.broadcasted_iota(jnp.int32, (SUB, cols), 0) + (lat * rows + b * SUB)
            gpos = growi.astype(jnp.float32)
            zdep = jnp.clip(float(k) - d_ref[k, near], 0.0, levels - 1.0)
            ydep = jnp.clip(gpos - d_ref[levels + k, near], 0.0, total_rows - 1.0)
            xrel = -d_ref[2 * levels + k, near]
            zb = jnp.floor(zdep)
            yb = jnp.floor(ydep)
            xb = jnp.floor(xrel)
            wz = spread(zb - 1.0, cubic_weights(zdep - zb), 0, levels - 1)
            wy = spread(yb - gpos - 1.0, cubic_weights(ydep - yb), -RIM, RIM)
            wx = spread(xb - 1.0, cubic_weights(xrel - xb), -RIM, RIM)

            def tracer(t, _):
                total = None
                for z in range(levels):
                    base = pl.multiple_of((t * levels + z) * high + b * SUB, SUB)
                    plane = None
                    for y in range(wide):
                        line = None
                        for x in range(wide):
                            term = wx[x] * shifted[x, pl.ds(base + y, SUB), :]
                            line = term if line is None else line + term
                        term = wy[y] * line
                        plane = term if plane is None else plane + term
                    term = wz[z] * plane
                    total = term if total is None else total + term
                result[t * levels + k, near] = total
                return 0

            lax.fori_loop(0, ntrac, tracer, 0)
    o_ref[...] = result[...].astype(o_ref.dtype)


def local(tracers, winds, zonal_shift):
    ntrac, levels, rows, cols = tracers.shape
    nlat = lax.axis_size("lat")
    nlon = lax.axis_size("lon")
    fields = ntrac * levels
    planes = 3 * levels
    high = rows + 2 * RIM
    dma = pltpu.SemaphoreType.DMA
    vmem = pl.BlockSpec(memory_space=pltpu.VMEM)
    any_space = pl.BlockSpec(memory_space=pl.ANY)
    by_row = jnp.transpose(tracers.reshape(fields, rows, cols), (1, 0, 2))
    pieces = rows // RIM
    gathered, shifts, disp = pl.pallas_call(
        functools.partial(exchange_kernel, nlat, nlon, levels),
        out_shape=(
            jax.ShapeDtypeStruct((nlon, high, fields, cols), tracers.dtype),
            jax.ShapeDtypeStruct((high, 1, 128), jnp.int32),
            jax.ShapeDtypeStruct((planes, rows, cols), jnp.float32),
        ),
        in_specs=[vmem, vmem, pl.BlockSpec(memory_space=pltpu.SMEM)],
        out_specs=(any_space, vmem, vmem),
        scratch_shapes=[
            pltpu.VMEM((rows, cols), jnp.float32),
            pltpu.VMEM((6, rows, cols), jnp.float32),
            pltpu.VMEM((planes, SUB, cols), jnp.float32),
            pltpu.VMEM((planes, SUB, cols), jnp.float32),
            pltpu.VMEM((5, planes, rows + 2 * SUB, cols), jnp.float32),
            dma((nlon, pieces)), dma((nlon, pieces)), dma((nlon,)), dma((nlon,)),
            dma((nlon, pieces)), dma((nlon,)), dma((nlon,)), dma,
            dma((8,)), dma((8,)), dma((2,)), dma((2,)),
        ],
        compiler_params=pltpu.CompilerParams(collective_id=0, has_side_effects=True),
        name="exchange",
    )(by_row, winds.reshape(planes, rows, cols), zonal_shift)
    out = pl.pallas_call(
        functools.partial(stencil_kernel, nlat, nlon, levels, rows),
        out_shape=jax.ShapeDtypeStruct((fields, rows, cols), tracers.dtype),
        in_specs=[pl.BlockSpec(memory_space=pltpu.SMEM), vmem, any_space],
        out_specs=vmem,
        scratch_shapes=[
            pltpu.VMEM((high, 3, fields, cols), tracers.dtype),
            pltpu.VMEM((2 * RIM + 1, fields * high, cols), jnp.float32),
            pltpu.VMEM((fields, rows, cols), jnp.float32),
            dma((high,)),
        ],
        name="stencil",
    )(shifts, disp, gathered)
    return out.reshape(tracers.shape), disp.reshape(winds.shape)


def solution(mesh):
    return jax.shard_map(
        local,
        mesh=mesh,
        in_specs=(P(None, None, "lat", "lon"), P(None, None, "lat", "lon"), P("lat")),
        out_specs=(P(None, None, "lat", "lon"), P(None, None, "lat", "lon")),
        check_vma=False,
    )
```

```python
import functools

import jax
import jax.numpy as jnp
from jax import lax
from jax.experimental import pallas as pl
from jax.experimental.pallas import tpu as pltpu
from jax.sharding import PartitionSpec as P

ITERS = 3
RIM = 4
SUB = 8
MESH = pl.DeviceIdType.MESH


def cubic_weights(frac):
    return (
        -frac * (frac - 1.0) * (frac - 2.0) / 6.0,
        (frac + 1.0) * (frac - 1.0) * (frac - 2.0) / 2.0,
        -(frac + 1.0) * frac * (frac - 2.0) / 2.0,
        (frac + 1.0) * frac * (frac - 1.0) / 6.0,
    )


def spread(base, weights, lowest, highest):
    listed = []
    for target in range(lowest, highest + 1):
        summed = jnp.zeros(base.shape, jnp.float32)
        for a in range(len(weights)):
            summed = summed + jnp.where(base == float(target - a), weights[a], 0.0)
        listed.append(summed)
    return listed


def exchange_kernel(
    nlat, nlon, levels, t_ref, w_ref, s_ref, g_ref, s_out, d_ref,
    edge, edges, wind_n, wind_s, wide,
    sem_z, sem_x, sem_n, sem_s, got, got_n, got_s, own_sem,
    sem_w, got_w, sem_i, got_i,
):
    rows, _, cols = t_ref.shape
    planes = w_ref.shape[0]
    lat = lax.axis_index("lat")
    lon = lax.axis_index("lon")
    zc = nlon // 2
    zi = lon // 2
    xi = lon % 2
    north = (lat + nlat - 1) % nlat
    south = (lat + 1) % nlat
    east = (lon + 1) % nlon
    west = (lon + nlon - 1) % nlon
    partner = zi * 2 + (1 - xi)

    def peer(j):
        return ((zi + j) % zc) * 2 + xi

    around = [(lat, east), (lat, west), (north, east), (north, west), (south, east), (south, west)]
    targets = [(north, lon), (south, lon), (lat, partner)] + around
    targets += [(lat, peer(j)) for j in range(1, zc)]
    barrier = pltpu.get_barrier_semaphore()
    for target in targets:
        pl.semaphore_signal(barrier, inc=1, device_id=target, device_id_type=MESH)

    lane = lax.broadcasted_iota(jnp.int32, (rows, cols), 1)
    packed = jnp.zeros((rows, cols), jnp.float32)
    for c in range(planes):
        turned = pltpu.roll(w_ref[c], (2 + 4 * c) % cols, 1)
        packed = jnp.where((lane >= 4 * c) & (lane < 4 * c + 4), turned, packed)
    edge[...] = packed
    for r in range(rows):
        s_out[RIM + r] = jnp.full(s_out.shape[1:], s_ref[r])
    pl.semaphore_wait(barrier, len(targets))

    def remote(src, dst, send, recv, target):
        copy = pltpu.make_async_remote_copy(
            src_ref=src, dst_ref=dst, send_sem=send, recv_sem=recv,
            device_id=target, device_id_type=MESH,
        )
        copy.start()
        return copy

    sends = []
    winds = []
    for n, target in enumerate(around):
        slot = (1, 0, 5, 4, 3, 2)[n]
        winds.append(remote(edge, edges.at[slot], sem_w.at[n], got_w.at[slot], target))
    winds.append(remote(w_ref.at[:, 0:SUB], wind_s, sem_w.at[6], got_w.at[6], (north, lon)))
    winds.append(remote(w_ref.at[:, rows - SUB : rows], wind_n, sem_w.at[7], got_w.at[7], (south, lon)))
    own_rows = s_out.at[RIM : RIM + rows]
    winds.append(remote(own_rows.at[0:RIM], s_out.at[RIM + rows : RIM + rows + RIM], sem_i.at[0], got_i.at[0], (north, lon)))
    winds.append(remote(own_rows.at[rows - RIM : rows], s_out.at[0:RIM], sem_i.at[1], got_i.at[1], (south, lon)))

    pieces = rows // RIM
    piece_order = [0, pieces - 1] + list(range(1, pieces - 1))
    order = [j for pair in zip(range(1, zc), range(zc - 1, 0, -1)) for j in pair][: zc - 1]

    def part(c):
        return pl.ds(RIM + c * RIM, RIM)

    def rims(p, c, src):
        if c == 0:
            sends.append(remote(src, g_ref.at[p, RIM + rows : RIM + rows + RIM], sem_n.at[p], got_n.at[p], (north, lon)))
        if c == pieces - 1:
            sends.append(remote(src, g_ref.at[p, 0:RIM], sem_s.at[p], got_s.at[p], (south, lon)))

    for c in piece_order:
        mine = t_ref.at[c * RIM : (c + 1) * RIM]
        sends.append(remote(mine, g_ref.at[lon, part(c)], sem_x.at[lon, c], got.at[lon, c], (lat, partner)))
        for j in order:
            sends.append(remote(mine, g_ref.at[lon, part(c)], sem_z.at[j, c], got.at[lon, c], (lat, peer(j))))
        rims(lon, c, mine)
    own = pltpu.make_async_copy(t_ref, g_ref.at[lon, RIM : RIM + rows], own_sem)
    own.start()

    def arrived(p, c):
        pltpu.make_async_remote_copy(
            src_ref=g_ref.at[p, part(c)], dst_ref=g_ref.at[p, part(c)], send_sem=own_sem, recv_sem=got.at[p, c],
            device_id=(lat, partner), device_id_type=MESH,
        ).wait_recv()

    def relay(c):
        for j in order:
            p = ((zi + zc - j) % zc) * 2 + xi
            arrived(p, c)
            piece = g_ref.at[p, part(c)]
            sends.append(remote(piece, piece, sem_x.at[p, c], got.at[p, c], (lat, partner)))
            rims(p, c, piece)

    def pass_rims(c):
        for j in [0] + order:
            p = ((zi + zc - j) % zc) * 2 + (1 - xi)
            arrived(p, c)
            rims(p, c, g_ref.at[p, part(c)])

    for copy in winds:
        copy.wait()

    tall = rows + 2 * SUB
    total_rows = rows * nlat
    tall_lane = lax.broadcasted_iota(jnp.int32, (tall, cols), 1)
    rowpos = lax.broadcasted_iota(jnp.int32, (tall, cols), 0) + (lat * rows - SUB)
    inside = (rowpos >= 0) & (rowpos < total_rows)
    from_east = jnp.concatenate([edges[2][rows - SUB :], edges[0], edges[4][:SUB]], axis=0)
    from_west = jnp.concatenate([edges[3][rows - SUB :], edges[1], edges[5][:SUB]], axis=0)
    for c in range(planes):
        block = jnp.concatenate([wind_n[c], w_ref[c], wind_s[c]], axis=0)
        for d in range(-2, 3):
            if d > 0:
                value = jnp.where(
                    tall_lane >= cols - d,
                    pltpu.roll(from_east, (cols - 2 - d - 4 * c) % cols, 1),
                    pltpu.roll(block, cols - d, 1),
                )
            elif d < 0:
                value = jnp.where(
                    tall_lane < -d,
                    pltpu.roll(from_west, (-d - 2 - 4 * c) % cols, 1),
                    pltpu.roll(block, -d, 1),
                )
            else:
                value = block
            wide[d + 2, c] = jnp.where(inside, value, 0.0)

    def trajectory(k):
        for b in range(rows // SUB):
            near = slice(b * SUB, (b + 1) * SUB)
            growi = lax.broadcasted_iota(jnp.int32, (SUB, cols), 0) + (lat * rows + b * SUB)
            gpos = growi.astype(jnp.float32)

            def step(_, disp):
                zlev = jnp.clip(float(k) - 0.5 * disp[0], 0.0, levels - 1.0)
                ylat = jnp.clip(gpos - 0.5 * disp[1], 0.0, total_rows - 1.0)
                xrel = -0.5 * disp[2]
                zb = jnp.floor(zlev)
                yb = jnp.floor(ylat)
                xb = jnp.floor(xrel)
                tz = zlev - zb
                ty = ylat - yb
                tx = xrel - xb
                wz = spread(zb, (1.0 - tz, tz), 0, levels - 1)
                wy = spread(yb - gpos, (1.0 - ty, ty), -2, 2)
                wx = spread(xb, (1.0 - tx, tx), -2, 2)
                result = []
                for comp in range(3):
                    total = None
                    for z in range(levels):
                        plane = None
                        for y in range(5):
                            start = SUB + b * SUB + y - 2
                            line = None
                            for x in range(5):
                                term = wx[x] * wide[x, comp * levels + z, start : start + SUB]
                                line = term if line is None else line + term
                            term = wy[y] * line
                            plane = term if plane is None else plane + term
                        term = wz[z] * plane
                        total = term if total is None else total + term
                    result.append(total)
                return tuple(result)

            disp = tuple(w_ref[comp * levels + k, near] for comp in range(3))
            disp = lax.fori_loop(0, ITERS, step, disp)
            for comp in range(3):
                d_ref[comp * levels + k, near] = disp[comp]

    for n in range(max(levels, pieces)):
        if n < levels:
            trajectory(n)
        if n < pieces:
            relay(piece_order[n])
            if n > 0:
                pass_rims(piece_order[n - 1])
    pass_rims(piece_order[-1])
    own.wait()
    for copy in sends:
        copy.wait_send()
    for p in range(nlon):
        for dst, sem in ((g_ref.at[p, RIM + rows : RIM + rows + RIM], got_n), (g_ref.at[p, 0:RIM], got_s)):
            pltpu.make_async_remote_copy(
                src_ref=dst, dst_ref=dst, send_sem=own_sem, recv_sem=sem.at[p],
                device_id=(north, lon), device_id_type=MESH,
            ).wait_recv()


def stencil_kernel(nlat, nlon, levels, rows, s_ref, d_ref, g_ref, o_ref, window, source, band, wxs, wys, wzs, partial_sum, result, sems):
    high, fields, cols = g_ref.shape[1:]
    ntrac = fields // levels
    pitch = source.shape[0] // high
    wide = 2 * RIM + 1
    turn_rows = band.shape[1]
    lat = lax.axis_index("lat")
    lon = lax.axis_index("lon")
    total_rows = rows * nlat

    def place(r):
        first = lon * cols - RIM - s_ref[r, 0, 0] + 2 * nlon * cols
        return first // cols, first % cols

    def start(r, _):
        base = place(r)[0]
        for n in range(3):
            pltpu.make_async_copy(g_ref.at[(base + n) % nlon, r], window.at[r, n], sems.at[r]).start()
        return 0

    lax.fori_loop(0, high, start, 0)

    gpos = (lax.broadcasted_iota(jnp.int32, (rows, cols), 0) + lat * rows).astype(jnp.float32)
    for k in range(levels):
        zdep = jnp.clip(float(k) - d_ref[k], 0.0, levels - 1.0)
        ydep = jnp.clip(gpos - d_ref[levels + k], 0.0, total_rows - 1.0)
        xrel = -d_ref[2 * levels + k]
        zb = jnp.floor(zdep)
        yb = jnp.floor(ydep)
        xb = jnp.floor(xrel)
        for z, value in enumerate(spread(zb - 1.0, cubic_weights(zdep - zb), 0, levels - 1)):
            wzs[k * levels + z] = value
        for y, value in enumerate(spread(yb - gpos - 1.0, cubic_weights(ydep - yb), -RIM, RIM)):
            wys[k * wide + y] = value
        for x, value in enumerate(spread(xb - 1.0, cubic_weights(xrel - xb), -RIM, RIM)):
            wxs[k, x * rows : (x + 1) * rows] = value
        for x in range(wide, turn_rows):
            wxs[k, x * rows : (x + 1) * rows] = jnp.zeros((rows, cols), jnp.float32)
    blocks = band.shape[0]
    row_at = lax.broadcasted_iota(jnp.int32, (turn_rows, cols), 0)
    col_at = lax.broadcasted_iota(jnp.int32, (turn_rows, cols), 1)
    for m in range(blocks):
        apart = row_at + m * turn_rows - col_at
        band[m] = jnp.where((apart >= 0) & (apart < turn_rows), 1.0, 0.0).astype(band.dtype)

    lane = lax.broadcasted_iota(jnp.int32, (fields, cols), 1)

    def turn(r, _):
        pltpu.make_async_copy(g_ref.at[0:3, r], window.at[r], sems.at[r]).wait()
        offset = place(r)[1]
        rowpos = lat * rows - RIM + r
        keep = jnp.full((fields, cols), (rowpos >= 0) & (rowpos < total_rows))
        amount = (cols - offset) % cols
        turned = [pltpu.roll(window[r, n].astype(jnp.float32), amount, 1) for n in range(3)]
        early = lane < cols - offset
        spare = jnp.zeros((pitch - fields, cols), jnp.float32)
        at = pl.ds(pl.multiple_of(r * pitch, pitch), pitch)
        for n in range(2):
            value = jnp.where(keep, jnp.where(early, turned[n], turned[n + 1]), 0.0)
            source[at, n * cols : (n + 1) * cols] = jnp.concatenate([value, spare], axis=0).astype(source.dtype)
        return 0

    lax.fori_loop(0, high, turn, 0)
    tail = jnp.zeros((2 * cols - blocks * turn_rows, 2 * cols), source.dtype)

    def row(i, _):
        near = source[pl.ds(pl.multiple_of(i * pitch, pitch), wide * pitch), :]
        for k in range(levels):
            turned = wxs[k, pl.ds(i, turn_rows, stride=rows), :]
            bit = 1
            while bit < turn_rows:
                turned = jnp.where((col_at & bit) != 0, pltpu.roll(turned, bit, 0), turned)
                bit *= 2
            head = turned.astype(source.dtype)
            rest = (turned - head.astype(jnp.float32)).astype(source.dtype)
            matrix = jnp.concatenate(
                [jnp.concatenate([head * band[m], rest * band[m]], axis=1) for m in range(blocks)] + [tail],
                axis=0,
            )
            lines = jnp.dot(near, matrix, preferred_element_type=jnp.float32)
            total = None
            for y in range(wide):
                line = lines[y * pitch : y * pitch + fields]
                term = wys[k * wide + y, pl.ds(i, 1), :] * (line[:, :cols] + line[:, cols:])
                total = term if total is None else total + term
            partial_sum[k] = total
            value = None
            for z in range(levels):
                term = wzs[k * levels + z, pl.ds(i, 1), :] * partial_sum[k, pl.ds(z, ntrac, stride=levels), :]
                value = term if value is None else value + term
            result[pl.ds(k * rows + i, ntrac, stride=levels * rows), :] = value
        return 0

    lax.fori_loop(0, rows, row, 0)
    o_ref[...] = result[...].reshape(o_ref.shape).astype(o_ref.dtype)


def local(tracers, winds, zonal_shift):
    ntrac, levels, rows, cols = tracers.shape
    nlat = lax.axis_size("lat")
    nlon = lax.axis_size("lon")
    fields = ntrac * levels
    planes = 3 * levels
    high = rows + 2 * RIM
    dma = pltpu.SemaphoreType.DMA
    vmem = pl.BlockSpec(memory_space=pltpu.VMEM)
    any_space = pl.BlockSpec(memory_space=pl.ANY)
    by_row = jnp.transpose(tracers.reshape(fields, rows, cols), (1, 0, 2))
    pieces = rows // RIM
    band = 16
    pitch = (fields + band - 1) // band * band
    gathered, shifts, disp = pl.pallas_call(
        functools.partial(exchange_kernel, nlat, nlon, levels),
        out_shape=(
            jax.ShapeDtypeStruct((nlon, high, fields, cols), tracers.dtype),
            jax.ShapeDtypeStruct((high, 1, 128), jnp.int32),
            jax.ShapeDtypeStruct((planes, rows, cols), jnp.float32),
        ),
        in_specs=[vmem, vmem, pl.BlockSpec(memory_space=pltpu.SMEM)],
        out_specs=(any_space, vmem, vmem),
        scratch_shapes=[
            pltpu.VMEM((rows, cols), jnp.float32),
            pltpu.VMEM((6, rows, cols), jnp.float32),
            pltpu.VMEM((planes, SUB, cols), jnp.float32),
            pltpu.VMEM((planes, SUB, cols), jnp.float32),
            pltpu.VMEM((5, planes, rows + 2 * SUB, cols), jnp.float32),
            dma((nlon, pieces)), dma((nlon, pieces)), dma((nlon,)), dma((nlon,)),
            dma((nlon, pieces)), dma((nlon,)), dma((nlon,)), dma,
            dma((8,)), dma((8,)), dma((2,)), dma((2,)),
        ],
        compiler_params=pltpu.CompilerParams(collective_id=0, has_side_effects=True),
        name="exchange",
    )(by_row, winds.reshape(planes, rows, cols), zonal_shift)
    out = pl.pallas_call(
        functools.partial(stencil_kernel, nlat, nlon, levels, rows),
        out_shape=jax.ShapeDtypeStruct((fields, rows, cols), tracers.dtype),
        in_specs=[pl.BlockSpec(memory_space=pltpu.SMEM), vmem, any_space],
        out_specs=vmem,
        scratch_shapes=[
            pltpu.VMEM((high, 3, fields, cols), tracers.dtype),
            pltpu.VMEM((high * pitch, 2 * cols), jnp.bfloat16),
            pltpu.VMEM(((cols + 2 * RIM + band - 1) // band, band, cols), jnp.bfloat16),
            pltpu.VMEM((levels, band * rows, cols), jnp.float32),
            pltpu.VMEM(((2 * RIM + 1) * levels, rows, cols), jnp.float32),
            pltpu.VMEM((levels * levels, rows, cols), jnp.float32),
            pltpu.VMEM((levels, fields, cols), jnp.float32),
            pltpu.VMEM((fields * rows, cols), jnp.float32),
            dma((high,)),
        ],
        name="stencil",
    )(shifts, disp, gathered)
    return out.reshape(tracers.shape), disp.reshape(winds.shape)


def solution(mesh):
    return jax.shard_map(
        local,
        mesh=mesh,
        in_specs=(P(None, None, "lat", "lon"), P(None, None, "lat", "lon"), P("lat")),
        out_specs=(P(None, None, "lat", "lon"), P(None, None, "lat", "lon")),
        check_vma=False,
    )
```

```python
import functools

import jax
import jax.numpy as jnp
from jax import lax
from jax.experimental import pallas as pl
from jax.experimental.pallas import tpu as pltpu
from jax.sharding import PartitionSpec as P

ITERS = 3
RIM = 4
SUB = 8
MESH = pl.DeviceIdType.MESH


def cubic_weights(frac):
    return (
        -frac * (frac - 1.0) * (frac - 2.0) / 6.0,
        (frac + 1.0) * (frac - 1.0) * (frac - 2.0) / 2.0,
        -(frac + 1.0) * frac * (frac - 2.0) / 2.0,
        (frac + 1.0) * frac * (frac - 1.0) / 6.0,
    )


def spread(base, weights, lowest, highest):
    listed = []
    for target in range(lowest, highest + 1):
        summed = jnp.zeros(base.shape, jnp.float32)
        for a in range(len(weights)):
            summed = summed + jnp.where(base == float(target - a), weights[a], 0.0)
        listed.append(summed)
    return listed


def exchange_kernel(
    nlat, nlon, levels, t_ref, w_ref, s_ref, g_ref, s_out, d_ref,
    edge, edges, wind_n, wind_s, wide,
    sem_z, sem_x, sem_n, sem_s, got, got_n, got_s, own_sem,
    sem_w, got_w, sem_i, got_i,
):
    rows, _, cols = t_ref.shape
    planes = w_ref.shape[0]
    lat = lax.axis_index("lat")
    lon = lax.axis_index("lon")
    zc = nlon // 2
    zi = lon // 2
    xi = lon % 2
    north = (lat + nlat - 1) % nlat
    south = (lat + 1) % nlat
    east = (lon + 1) % nlon
    west = (lon + nlon - 1) % nlon
    partner = zi * 2 + (1 - xi)

    def peer(j):
        return ((zi + j) % zc) * 2 + xi

    around = [(lat, east), (lat, west), (north, east), (north, west), (south, east), (south, west)]
    targets = [(north, lon), (south, lon), (lat, partner)] + around
    targets += [(lat, peer(j)) for j in range(1, zc)]
    barrier = pltpu.get_barrier_semaphore()
    for target in targets:
        pl.semaphore_signal(barrier, inc=1, device_id=target, device_id_type=MESH)

    lane = lax.broadcasted_iota(jnp.int32, (rows, cols), 1)
    packed = jnp.zeros((rows, cols), jnp.float32)
    for c in range(planes):
        turned = pltpu.roll(w_ref[c], (2 + 4 * c) % cols, 1)
        packed = jnp.where((lane >= 4 * c) & (lane < 4 * c + 4), turned, packed)
    edge[...] = packed
    for r in range(rows):
        s_out[RIM + r] = jnp.full(s_out.shape[1:], s_ref[r])
    pl.semaphore_wait(barrier, len(targets))

    def remote(src, dst, send, recv, target):
        copy = pltpu.make_async_remote_copy(
            src_ref=src, dst_ref=dst, send_sem=send, recv_sem=recv,
            device_id=target, device_id_type=MESH,
        )
        copy.start()
        return copy

    sends = []
    winds = []
    for n, target in enumerate(around):
        slot = (1, 0, 5, 4, 3, 2)[n]
        winds.append(remote(edge, edges.at[slot], sem_w.at[n], got_w.at[slot], target))
    winds.append(remote(w_ref.at[:, 0:SUB], wind_s, sem_w.at[6], got_w.at[6], (north, lon)))
    winds.append(remote(w_ref.at[:, rows - SUB : rows], wind_n, sem_w.at[7], got_w.at[7], (south, lon)))
    own_rows = s_out.at[RIM : RIM + rows]
    winds.append(remote(own_rows.at[0:RIM], s_out.at[RIM + rows : RIM + rows + RIM], sem_i.at[0], got_i.at[0], (north, lon)))
    winds.append(remote(own_rows.at[rows - RIM : rows], s_out.at[0:RIM], sem_i.at[1], got_i.at[1], (south, lon)))

    pieces = rows // RIM
    piece_order = [0, pieces - 1] + list(range(1, pieces - 1))
    order = [j for pair in zip(range(1, zc), range(zc - 1, 0, -1)) for j in pair][: zc - 1]

    def part(c):
        return pl.ds(RIM + c * RIM, RIM)

    def rims(p, c, src):
        if c == 0:
            sends.append(remote(src, g_ref.at[p, RIM + rows : RIM + rows + RIM], sem_n.at[p], got_n.at[p], (north, lon)))
        if c == pieces - 1:
            sends.append(remote(src, g_ref.at[p, 0:RIM], sem_s.at[p], got_s.at[p], (south, lon)))

    for c in piece_order:
        mine = t_ref.at[c * RIM : (c + 1) * RIM]
        sends.append(remote(mine, g_ref.at[lon, part(c)], sem_x.at[lon, c], got.at[lon, c], (lat, partner)))
        for j in order:
            sends.append(remote(mine, g_ref.at[lon, part(c)], sem_z.at[j, c], got.at[lon, c], (lat, peer(j))))
        rims(lon, c, mine)
    own = pltpu.make_async_copy(t_ref, g_ref.at[lon, RIM : RIM + rows], own_sem)
    own.start()

    def arrived(p, c):
        pltpu.make_async_remote_copy(
            src_ref=g_ref.at[p, part(c)], dst_ref=g_ref.at[p, part(c)], send_sem=own_sem, recv_sem=got.at[p, c],
            device_id=(lat, partner), device_id_type=MESH,
        ).wait_recv()

    def relay(c):
        for j in order:
            p = ((zi + zc - j) % zc) * 2 + xi
            arrived(p, c)
            piece = g_ref.at[p, part(c)]
            sends.append(remote(piece, piece, sem_x.at[p, c], got.at[p, c], (lat, partner)))
            rims(p, c, piece)

    def pass_rims(c):
        for j in [0] + order:
            p = ((zi + zc - j) % zc) * 2 + (1 - xi)
            arrived(p, c)
            rims(p, c, g_ref.at[p, part(c)])

    for copy in winds:
        copy.wait()

    tall = rows + 2 * SUB
    total_rows = rows * nlat
    tall_lane = lax.broadcasted_iota(jnp.int32, (tall, cols), 1)
    rowpos = lax.broadcasted_iota(jnp.int32, (tall, cols), 0) + (lat * rows - SUB)
    inside = (rowpos >= 0) & (rowpos < total_rows)
    from_east = jnp.concatenate([edges[2][rows - SUB :], edges[0], edges[4][:SUB]], axis=0)
    from_west = jnp.concatenate([edges[3][rows - SUB :], edges[1], edges[5][:SUB]], axis=0)
    for c in range(planes):
        block = jnp.concatenate([wind_n[c], w_ref[c], wind_s[c]], axis=0)
        for d in range(-2, 3):
            if d > 0:
                value = jnp.where(
                    tall_lane >= cols - d,
                    pltpu.roll(from_east, (cols - 2 - d - 4 * c) % cols, 1),
                    pltpu.roll(block, cols - d, 1),
                )
            elif d < 0:
                value = jnp.where(
                    tall_lane < -d,
                    pltpu.roll(from_west, (-d - 2 - 4 * c) % cols, 1),
                    pltpu.roll(block, -d, 1),
                )
            else:
                value = block
            wide[d + 2, c] = jnp.where(inside, value, 0.0)

    def trajectory(k):
        for b in range(rows // SUB):
            near = slice(b * SUB, (b + 1) * SUB)
            growi = lax.broadcasted_iota(jnp.int32, (SUB, cols), 0) + (lat * rows + b * SUB)
            gpos = growi.astype(jnp.float32)

            def step(_, disp):
                zlev = jnp.clip(float(k) - 0.5 * disp[0], 0.0, levels - 1.0)
                ylat = jnp.clip(gpos - 0.5 * disp[1], 0.0, total_rows - 1.0)
                xrel = -0.5 * disp[2]
                zb = jnp.floor(zlev)
                yb = jnp.floor(ylat)
                xb = jnp.floor(xrel)
                tz = zlev - zb
                ty = ylat - yb
                tx = xrel - xb
                wz = spread(zb, (1.0 - tz, tz), 0, levels - 1)
                wy = spread(yb - gpos, (1.0 - ty, ty), -2, 2)
                wx = spread(xb, (1.0 - tx, tx), -2, 2)
                result = []
                for comp in range(3):
                    total = None
                    for z in range(levels):
                        plane = None
                        for y in range(5):
                            start = SUB + b * SUB + y - 2
                            line = None
                            for x in range(5):
                                term = wx[x] * wide[x, comp * levels + z, start : start + SUB]
                                line = term if line is None else line + term
                            term = wy[y] * line
                            plane = term if plane is None else plane + term
                        term = wz[z] * plane
                        total = term if total is None else total + term
                    result.append(total)
                return tuple(result)

            disp = tuple(w_ref[comp * levels + k, near] for comp in range(3))
            disp = lax.fori_loop(0, ITERS, step, disp)
            for comp in range(3):
                d_ref[comp * levels + k, near] = disp[comp]

    for n in range(max(levels, pieces)):
        if n < levels:
            trajectory(n)
        if n < pieces:
            relay(piece_order[n])
            if n > 0:
                pass_rims(piece_order[n - 1])
    pass_rims(piece_order[-1])
    own.wait()
    for copy in sends:
        copy.wait_send()
    for p in range(nlon):
        for dst, sem in ((g_ref.at[p, RIM + rows : RIM + rows + RIM], got_n), (g_ref.at[p, 0:RIM], got_s)):
            pltpu.make_async_remote_copy(
                src_ref=dst, dst_ref=dst, send_sem=own_sem, recv_sem=sem.at[p],
                device_id=(north, lon), device_id_type=MESH,
            ).wait_recv()


def stencil_kernel(nlat, nlon, levels, rows, s_ref, d_ref, g_ref, o_ref, d_out, window, source, band, wxs, wys, wzs, partial_sum, result, sems):
    high, fields, cols = g_ref.shape[1:]
    ntrac = fields // levels
    pitch = source.shape[0] // high
    wide = 2 * RIM + 1
    turn_rows = band.shape[1]
    lat = lax.axis_index("lat")
    lon = lax.axis_index("lon")
    total_rows = rows * nlat

    def place(r):
        first = lon * cols - RIM - s_ref[r, 0, 0] + 2 * nlon * cols
        return first // cols, first % cols

    def start(r, _):
        base = place(r)[0]
        for n in range(3):
            pltpu.make_async_copy(g_ref.at[(base + n) % nlon, r], window.at[r, n], sems.at[r]).start()
        return 0

    lax.fori_loop(0, high, start, 0)

    d_out[...] = d_ref[...]
    gpos = (lax.broadcasted_iota(jnp.int32, (rows, cols), 0) + lat * rows).astype(jnp.float32)
    for k in range(levels):
        zdep = jnp.clip(float(k) - d_ref[k], 0.0, levels - 1.0)
        ydep = jnp.clip(gpos - d_ref[levels + k], 0.0, total_rows - 1.0)
        xrel = -d_ref[2 * levels + k]
        zb = jnp.floor(zdep)
        yb = jnp.floor(ydep)
        xb = jnp.floor(xrel)
        for z, value in enumerate(spread(zb - 1.0, cubic_weights(zdep - zb), 0, levels - 1)):
            wzs[k * levels + z] = value
        for y, value in enumerate(spread(yb - gpos - 1.0, cubic_weights(ydep - yb), -RIM, RIM)):
            wys[k * wide + y] = value
        for x, value in enumerate(spread(xb - 1.0, cubic_weights(xrel - xb), -RIM, RIM)):
            wxs[k, x * rows : (x + 1) * rows] = value
        for x in range(wide, turn_rows):
            wxs[k, x * rows : (x + 1) * rows] = jnp.zeros((rows, cols), jnp.float32)
    blocks = band.shape[0]
    row_at = lax.broadcasted_iota(jnp.int32, (turn_rows, cols), 0)
    col_at = lax.broadcasted_iota(jnp.int32, (turn_rows, cols), 1)
    for m in range(blocks):
        apart = row_at + m * turn_rows - col_at
        band[m] = jnp.where((apart >= 0) & (apart < turn_rows), 1.0, 0.0).astype(band.dtype)

    lane = lax.broadcasted_iota(jnp.int32, (fields, cols), 1)

    def turn(r, _):
        pltpu.make_async_copy(g_ref.at[0:3, r], window.at[r], sems.at[r]).wait()
        offset = place(r)[1]
        rowpos = lat * rows - RIM + r
        keep = jnp.full((fields, cols), (rowpos >= 0) & (rowpos < total_rows))
        amount = (cols - offset) % cols
        turned = [pltpu.roll(window[r, n].astype(jnp.float32), amount, 1) for n in range(3)]
        early = lane < cols - offset
        spare = jnp.zeros((pitch - fields, cols), jnp.float32)
        at = pl.ds(pl.multiple_of(r * pitch, pitch), pitch)
        for n in range(2):
            value = jnp.where(keep, jnp.where(early, turned[n], turned[n + 1]), 0.0)
            source[at, n * cols : (n + 1) * cols] = jnp.concatenate([value, spare], axis=0).astype(source.dtype)
        return 0

    lax.fori_loop(0, high, turn, 0, unroll=4)
    tail = jnp.zeros((2 * cols - blocks * turn_rows, 2 * cols), source.dtype)

    def row(i, _):
        near = source[pl.ds(pl.multiple_of(i * pitch, pitch), wide * pitch), :]
        for k in range(levels):
            turned = wxs[k, pl.ds(i, turn_rows, stride=rows), :]
            bit = 1
            while bit < turn_rows:
                turned = jnp.where((col_at & bit) != 0, pltpu.roll(turned, bit, 0), turned)
                bit *= 2
            head = turned.astype(source.dtype)
            rest = (turned - head.astype(jnp.float32)).astype(source.dtype)
            matrix = jnp.concatenate(
                [jnp.concatenate([head * band[m], rest * band[m]], axis=1) for m in range(blocks)] + [tail],
                axis=0,
            )
            lines = jnp.dot(near, matrix, preferred_element_type=jnp.float32)
            total = None
            for y in range(wide):
                line = lines[y * pitch : y * pitch + fields]
                term = wys[k * wide + y, pl.ds(i, 1), :] * (line[:, :cols] + line[:, cols:])
                total = term if total is None else total + term
            partial_sum[k] = total
            value = None
            for z in range(levels):
                term = wzs[k * levels + z, pl.ds(i, 1), :] * partial_sum[k, pl.ds(z, ntrac, stride=levels), :]
                value = term if value is None else value + term
            result[pl.ds(k * rows + i, ntrac, stride=levels * rows), :] = value
        return 0

    lax.fori_loop(0, rows, row, 0, unroll=2)
    o_ref[...] = result[...].reshape(o_ref.shape).astype(o_ref.dtype)


def local(tracers, winds, zonal_shift):
    ntrac, levels, rows, cols = tracers.shape
    nlat = lax.axis_size("lat")
    nlon = lax.axis_size("lon")
    fields = ntrac * levels
    planes = 3 * levels
    high = rows + 2 * RIM
    dma = pltpu.SemaphoreType.DMA
    vmem = pl.BlockSpec(memory_space=pltpu.VMEM)
    any_space = pl.BlockSpec(memory_space=pl.ANY)
    by_row = jnp.transpose(tracers.reshape(fields, rows, cols), (1, 0, 2))
    pieces = rows // RIM
    band = 16
    pitch = (fields + band - 1) // band * band
    gathered, shifts, disp = pl.pallas_call(
        functools.partial(exchange_kernel, nlat, nlon, levels),
        out_shape=(
            jax.ShapeDtypeStruct((nlon, high, fields, cols), tracers.dtype),
            jax.ShapeDtypeStruct((high, 1, 128), jnp.int32),
            jax.ShapeDtypeStruct((planes, rows, cols), jnp.float32),
        ),
        in_specs=[vmem, vmem, pl.BlockSpec(memory_space=pltpu.SMEM)],
        out_specs=(any_space, vmem, vmem),
        scratch_shapes=[
            pltpu.VMEM((rows, cols), jnp.float32),
            pltpu.VMEM((6, rows, cols), jnp.float32),
            pltpu.VMEM((planes, SUB, cols), jnp.float32),
            pltpu.VMEM((planes, SUB, cols), jnp.float32),
            pltpu.VMEM((5, planes, rows + 2 * SUB, cols), jnp.float32),
            dma((nlon, pieces)), dma((nlon, pieces)), dma((nlon,)), dma((nlon,)),
            dma((nlon, pieces)), dma((nlon,)), dma((nlon,)), dma,
            dma((8,)), dma((8,)), dma((2,)), dma((2,)),
        ],
        compiler_params=pltpu.CompilerParams(collective_id=0, has_side_effects=True),
        name="exchange",
    )(by_row, winds.reshape(planes, rows, cols), zonal_shift)
    out, disp = pl.pallas_call(
        functools.partial(stencil_kernel, nlat, nlon, levels, rows),
        out_shape=(
            jax.ShapeDtypeStruct((fields, rows, cols), tracers.dtype),
            jax.ShapeDtypeStruct((planes, rows, cols), jnp.float32),
        ),
        in_specs=[pl.BlockSpec(memory_space=pltpu.SMEM), vmem, any_space],
        out_specs=(vmem, vmem),
        scratch_shapes=[
            pltpu.VMEM((high, 3, fields, cols), tracers.dtype),
            pltpu.VMEM((high * pitch, 2 * cols), jnp.bfloat16),
            pltpu.VMEM(((cols + 2 * RIM + band - 1) // band, band, cols), jnp.bfloat16),
            pltpu.VMEM((levels, band * rows, cols), jnp.float32),
            pltpu.VMEM(((2 * RIM + 1) * levels, rows, cols), jnp.float32),
            pltpu.VMEM((levels * levels, rows, cols), jnp.float32),
            pltpu.VMEM((levels, fields, cols), jnp.float32),
            pltpu.VMEM((fields * rows, cols), jnp.float32),
            dma((high,)),
        ],
        name="stencil",
    )(shifts, disp, gathered)
    return out.reshape(tracers.shape), disp.reshape(winds.shape)


def solution(mesh):
    return jax.shard_map(
        local,
        mesh=mesh,
        in_specs=(P(None, None, "lat", "lon"), P(None, None, "lat", "lon"), P("lat")),
        out_specs=(P(None, None, "lat", "lon"), P(None, None, "lat", "lon")),
        check_vma=False,
    )
```
